256 devices in a mesh: spec: 4 (over x), geo: 64 (over y, z, core).
Axes of the slice: x: 4, y: 4, z: 8, core: 2. Of those that a mesh axis runs over, the one named last changes fastest.
Arguments:
- spectrum: bfloat16 [1296, 1024, 128], P('spec', 'geo'), may hold values from 0.01 to 11, as said below
- sea_map: int32 [1024, 128], P('geo'), may hold values 0 or 1
- depth_factor: float32 [1024, 128], P('geo'), may hold values from 0.25 to 1
- wind_speed: bfloat16 [1024, 128], P('geo'), may hold values from 0.19921875 to 2
- wind_dir: bfloat16 [1024, 128], P('geo'), may hold values from -3.140625 to 3.140625
- ice_mask: int32 [1024, 128], P('geo'), may hold values from 0 to 1, as said below
- owner_map: int32 [1024, 128], P('geo'), may hold values from 0 to 63, as said below
- pair_kernel: bfloat16 [1296, 1296], replicated, may hold values from -1 to 2
- transfer_kernel: bfloat16 [64, 1296, 1296], P('geo'), may hold values from -1 to 2
Outputs:
- updated: bfloat16 [1296, 1024, 128], P('spec', 'geo')
The draws below stay inside these ranges and needn't reach their ends.
Inputs may be any that keep to these rules, and one draw needn't show every extreme that they name: `owner_map`: in each aligned block of 512 cells of the grid in row-major order, no owner is named by more than 16 cells, and one owner, the same in every block, is named by exactly 16 cells of each block. `ice_mask`: 1 marks ice. Cells of the owner that is named by 16 cells of every block are free of ice. `spectrum`: Positive.
All inputs are finite; a program needn't handle non-finite values. No bound on the sum of `sea_map` on one device may be relied on, other than what follows from the above.
Results may differ from the reference program's by a relative error of at most 0.0059.
Values may be sent and summed in bfloat16 or wider, within the bound.
A program may use at most 64 MiB of HBM per device.

```python
import math
import jax
import jax.numpy as jnp
from jax import lax

NDIR = 36
NFREQ = 36
COMP = 1296
CY = 128
NX = 1024
ROWS_DEV = 512
CAP = 16
TILES = 64


def routing_tables(key):
    base = jax.random.fold_in(key, 7001)
    key_hot, key_blocks, key_ice = jax.random.split(base, 3)
    block_count = NX * CY // ROWS_DEV
    hottest = jax.random.randint(key_hot, (), 0, TILES).astype(jnp.int32)
    spread_rows = ROWS_DEV - CAP
    others = TILES - 1
    levels = jnp.arange(others + 1, dtype=jnp.int32)
    bounds = spread_rows * (17 * levels * others - 7 * levels * levels) // (10 * others * others)
    position = jnp.arange(ROWS_DEV, dtype=jnp.int32)
    shifted = position - CAP
    tier = jnp.sum((bounds[None, 1:] <= shifted[:, None]).astype(jnp.int32), axis=1)
    tier = jnp.minimum(tier, others - 1)

    def one_block(block_key):
        key_order, key_place = jax.random.split(block_key)
        order = jax.random.permutation(key_order, others).astype(jnp.int32)
        chosen = (hottest + 1 + order[tier]) % TILES
        ranked = jnp.where(position < CAP, hottest, chosen).astype(jnp.int32)
        placed = jax.random.permutation(key_place, ROWS_DEV)
        return jnp.zeros((ROWS_DEV,), jnp.int32).at[placed].set(ranked)
    owners = jax.vmap(one_block)(jax.random.split(key_blocks, block_count)).reshape(NX, CY)
    frozen = jax.random.randint(key_ice, (NX, CY), 0, 8) == 0
    ice = jnp.where(frozen & (owners != hottest), 1, 0).astype(jnp.int32)
    return (owners.astype(jnp.int32), ice)


def draw_owner_map(key, part):
    owners, ice = routing_tables(key)
    return owners


def draw_ice_mask(key, part):
    owners, ice = routing_tables(key)
    return ice


def draw_spectrum(key, part):
    base = jax.random.fold_in(key, 7101)
    key_cell, key_profile, key_rough = jax.random.split(base, 3)
    cell_scale = jnp.exp(jax.random.uniform(key_cell, (1, NX, CY), jnp.float32, math.log(0.2), math.log(2.0)))
    profile = jnp.exp(jax.random.uniform(key_profile, (COMP, 1, 1), jnp.float32, math.log(0.3), math.log(3.0)))
    rough = jax.random.uniform(key_rough, (COMP, NX, CY), jnp.float32, 0.5, 1.5)
    return (cell_scale * profile * rough).astype(jnp.bfloat16)


def kernel_matrix(key, leading, off_scale):
    key_diag, key_off = jax.random.split(key)
    diagonal = jax.random.uniform(key_diag, leading + (COMP,), jnp.float32, 0.5, 1.5)
    off_part = jax.random.truncated_normal(key_off, -3.0, 3.0, leading + (COMP, COMP), jnp.float32)
    index = jnp.arange(COMP, dtype=jnp.int32)
    identity = (index[:, None] == index[None, :]).astype(jnp.float32)
    return identity * diagonal[..., :, None] + off_part * (off_scale / math.sqrt(COMP))


def draw_pair_kernel(key, part):
    return kernel_matrix(jax.random.fold_in(key, 7201), (), 0.8).astype(jnp.bfloat16)


def draw_transfer_kernel(key, part):
    return kernel_matrix(jax.random.fold_in(key, 7301), (TILES,), 0.6).astype(jnp.bfloat16)


def with_ends(values, stream_key, smallest, largest):
    longest = values.shape.index(max(values.shape))
    spots = []
    for shift in (0, 1):
        where = [jax.random.randint(jax.random.fold_in(stream_key, axis), (), 0, length) for axis, length in enumerate(values.shape)]
        where[longest] = (where[longest] + shift) % values.shape[longest]
        spots.append(tuple(where))
    return values.at[spots[0]].set(smallest).at[spots[1]].set(largest)


def block_scale(rng, dims, pieces, low, top_value):
    loudness = 1.0
    for dim, shards_of in pieces:
        heights = jax.random.uniform(jax.random.fold_in(jax.random.fold_in(rng, 6), dim), (shards_of,), jnp.float32, low / len(pieces), top_value / len(pieces))
        loudness = loudness * jnp.repeat(jnp.exp(heights), dims[dim] // shards_of).reshape((-1,) + (1,) * (len(dims) - 1 - dim))
    return loudness


def setup_inputs(seed: int = 0) -> dict:
    key_list = jax.random.split(jax.random.key(seed), 10)
    return {
        "spectrum": draw_spectrum(jax.random.fold_in(key_list[9], 71), 0),
        "sea_map": with_ends((jax.random.randint(key_list[1], (NX, CY), 0, 8) < 7).astype(jnp.int32), jax.random.fold_in(key_list[1], 1), 0, 1),
        "depth_factor": jnp.clip(jnp.exp(math.log(1.0) - 1.3862944 * jax.random.uniform(key_list[2], (NX, CY), jnp.float32) ** block_scale(key_list[2], (NX, CY), ((0, 64),), -0.2, 0.2)), 0.25, 1.0),
        "wind_speed": jnp.clip(jnp.exp(math.log(2.0) - 2.306499 * jax.random.uniform(key_list[3], (NX, CY), jnp.float32) ** block_scale(key_list[3], (NX, CY), ((0, 64),), -0.2, 0.2)), 0.19921875, 2.0).astype(jnp.bfloat16),
        "wind_dir": jnp.clip(jax.random.uniform(key_list[4], (NX, CY), jnp.float32, -3.140625, 3.140625), -3.140625, 3.140625).astype(jnp.bfloat16),
        "ice_mask": draw_ice_mask(jax.random.fold_in(key_list[9], 71), 0),
        "owner_map": draw_owner_map(jax.random.fold_in(key_list[9], 71), 0),
        "pair_kernel": draw_pair_kernel(jax.random.fold_in(key_list[9], 71), 0),
        "transfer_kernel": draw_transfer_kernel(jax.random.fold_in(key_list[9], 71), 0),
    }


def finish(row_data, transfer, wind_rows, wind_angle):
    energy = row_data.astype(jnp.float32)
    total = jnp.mean(energy, axis=0)
    ratio = total / (1.0 + total)
    component = jnp.arange(row_data.shape[0], dtype=jnp.int32)
    heading = 2.0 * math.pi * ((component % NDIR).astype(jnp.float32) + 0.5) / NDIR
    forcing = 0.3 * wind_rows.astype(jnp.float32)[None, :] * jnp.maximum(jnp.cos(heading[:, None] - wind_angle.astype(jnp.float32)[None, :]), 0.0)
    result = energy * (1.0 + forcing - 0.5 * ratio[None, :]) + 0.2 * transfer.astype(jnp.float32) / (1.0 + total)[None, :]
    return result.astype(jnp.bfloat16)


def propagate(spectrum, sea_map, depth_factor):
    sea_weight = sea_map.astype(jnp.float32)
    depth_cell = depth_factor.astype(jnp.float32)
    heading = 2.0 * math.pi * (jnp.arange(NDIR, dtype=jnp.int32).astype(jnp.float32) + 0.5) / NDIR
    cosine = jnp.cos(heading)[:, None, None]
    sine = jnp.sin(heading)[:, None, None]
    bands = spectrum.reshape(NFREQ, NDIR, NX, CY)
    frequency = jnp.arange(NFREQ, dtype=jnp.int32).astype(jnp.float32)

    def advect_band(item):
        band_freq, band = item
        centre = band.astype(jnp.float32) * sea_weight
        gain = jnp.float32(1.1) ** (-0.5 * band_freq)
        step_x = 0.7 * gain * jnp.abs(cosine) * depth_cell
        step_y = 0.7 * gain * jnp.abs(sine) * depth_cell
        zeros_x = jnp.zeros((NDIR, 1, CY), jnp.float32)
        zeros_y = jnp.zeros((NDIR, NX, 1), jnp.float32)
        west_side = jnp.concatenate([zeros_x, centre[:, :-1]], axis=1)
        east_side = jnp.concatenate([centre[:, 1:], zeros_x], axis=1)
        south_side = jnp.concatenate([zeros_y, centre[:, :, :-1]], axis=2)
        north_side = jnp.concatenate([centre[:, :, 1:], zeros_y], axis=2)
        upwind_x = jnp.where(cosine > 0, west_side, east_side)
        upwind_y = jnp.where(sine > 0, south_side, north_side)
        advected = centre - step_x * (centre - upwind_x) - step_y * (centre - upwind_y)
        return (advected * sea_weight).astype(jnp.bfloat16)

    return lax.map(advect_band, (frequency, bands)).reshape(COMP, NX * CY)


def slot_numbers(owners):
    onehot = (owners[:, None] == jnp.arange(TILES, dtype=jnp.int32)[None, :]).astype(jnp.int32)
    before = jnp.cumsum(onehot, axis=0) - onehot
    position = jnp.sum(before * onehot, axis=1)
    return (owners * CAP + position).astype(jnp.int32)


def reference(spectrum, sea_map, depth_factor, wind_speed, wind_dir, ice_mask, owner_map, pair_kernel, transfer_kernel):
    block_count = NX * CY // ROWS_DEV
    propagated = propagate(spectrum, sea_map, depth_factor)
    blocks = propagated.reshape(COMP, block_count, ROWS_DEV).transpose(1, 0, 2)
    owner_blocks = owner_map.reshape(block_count, ROWS_DEV)
    slot_blocks = lax.map(slot_numbers, owner_blocks)

    def pair_block(item):
        row_data, slot_index = item
        coupled = jnp.dot(pair_kernel, row_data, preferred_element_type=jnp.float32)
        paired = (row_data.astype(jnp.float32) * coupled).astype(jnp.bfloat16)
        return jnp.zeros((COMP, TILES * CAP), jnp.bfloat16).at[:, slot_index].set(paired)

    packed = lax.map(pair_block, (blocks, slot_blocks))
    per_owner = packed.reshape(block_count, COMP, TILES, CAP).transpose(2, 1, 0, 3).reshape(TILES, COMP, block_count * CAP)

    def apply_kernel(item):
        own_kernel, columns = item
        return jnp.dot(own_kernel, columns, preferred_element_type=jnp.float32).astype(jnp.bfloat16)

    transfer = lax.map(apply_kernel, (transfer_kernel, per_owner))
    returned = transfer.reshape(TILES, COMP, block_count, CAP).transpose(2, 1, 0, 3).reshape(block_count, COMP, TILES * CAP)

    def finish_block(item):
        row_data, slot_index, back_block, frozen, wind_rows, wind_angle = item
        terms = back_block[:, slot_index]
        sourced = finish(row_data, terms, wind_rows, wind_angle)
        return jnp.where(frozen[None, :] == 1, row_data, sourced)

    finished = lax.map(finish_block, (blocks, slot_blocks, returned, ice_mask.reshape(block_count, ROWS_DEV), wind_speed.reshape(block_count, ROWS_DEV), wind_dir.reshape(block_count, ROWS_DEV)))
    return finished.transpose(1, 0, 2).reshape(COMP, NX, CY)
```

```python
import math

import jax
import jax.numpy as jnp
from jax import lax
from jax.sharding import PartitionSpec as P

NDIR = 36
BOTH = ("spec", "geo")


def padded_2(cells, sides, width):
    for axis, dim in sides:
        count = lax.axis_size(axis)
        ends = count - 1
        head = lax.slice_in_dim(cells, 0, width, axis=dim)
        tail = lax.slice_in_dim(cells, cells.shape[dim] - width, cells.shape[dim], axis=dim)
        cells = jnp.concatenate(
            [
                lax.ppermute(tail, axis, [(i, (i + 1) % count) for i in range(ends)]),
                cells,
                lax.ppermute(head, axis, [((i + 1) % count, i) for i in range(ends)]),
            ],
            axis=dim,
        )
    return cells


def finish(energy_bf, transfer, wind_rows, wind_angle):
    energy = energy_bf.astype(jnp.float32)
    total = jnp.mean(energy, axis=1)
    ratio = total / (1.0 + total)
    component = jnp.arange(energy_bf.shape[1], dtype=jnp.int32)
    heading = 2.0 * math.pi * ((component % NDIR).astype(jnp.float32) + 0.5) / NDIR
    forcing = (
        0.3
        * wind_rows.astype(jnp.float32)[:, None]
        * jnp.maximum(jnp.cos(heading[None, :] - wind_angle.astype(jnp.float32)[:, None]), 0.0)
    )
    result = (
        energy * (1.0 + forcing - 0.5 * ratio[:, None])
        + 0.2 * transfer.astype(jnp.float32) / (1.0 + total)[:, None]
    )
    return result.astype(jnp.bfloat16)


def per_device(
    spectrum,
    sea_map,
    depth_factor,
    wind_speed,
    wind_dir,
    ice_mask,
    owner_map,
    pair_kernel,
    transfer_kernel,
):
    comp_dev, cells_x, cells_y = spectrum.shape
    spec_count = lax.axis_size("spec")
    geo_count = lax.axis_size("geo")
    cells_dev = cells_x * cells_y
    rows_dev = cells_dev // spec_count
    capacity = 2 * rows_dev // geo_count
    slot_count = geo_count * capacity
    width = ((comp_dev + 2 + 3) // 4) * 4

    masked = spectrum * sea_map.astype(jnp.bfloat16)[None, :, :]
    padded = padded_2(masked, (("geo", 1),), 1)
    extended = padded.astype(jnp.float32)
    component = lax.axis_index("spec") * comp_dev + jnp.arange(comp_dev, dtype=jnp.int32)
    frequency = (component // NDIR).astype(jnp.float32)
    heading = 2.0 * math.pi * ((component % NDIR).astype(jnp.float32) + 0.5) / NDIR
    cosine = jnp.cos(heading)[:, None, None]
    sine = jnp.sin(heading)[:, None, None]
    gain = (jnp.float32(1.1) ** (-0.5 * frequency))[:, None, None]
    sea_weight = sea_map.astype(jnp.float32)
    step_x = 0.7 * gain * jnp.abs(cosine) * depth_factor
    step_y = 0.7 * gain * jnp.abs(sine) * depth_factor
    centre = extended[:, 1:-1]
    west_side = extended[:, :-2]
    east_side = extended[:, 2:]
    zeros_y = jnp.zeros((comp_dev, cells_x, 1), jnp.float32)
    south_side = jnp.concatenate([zeros_y, centre[:, :, :-1]], axis=2)
    north_side = jnp.concatenate([centre[:, :, 1:], zeros_y], axis=2)
    upwind_x = jnp.where(cosine > 0, west_side, east_side)
    upwind_y = jnp.where(sine > 0, south_side, north_side)
    advected = centre - step_x * (centre - upwind_x) - step_y * (centre - upwind_y)
    propagated = (advected * sea_weight).astype(jnp.bfloat16)
    prop_cells = propagated.reshape(comp_dev, cells_dev).T

    owners = owner_map.reshape(spec_count, rows_dev)
    is_live = 1 - ice_mask.reshape(spec_count, rows_dev)
    onehot = (owners[:, :, None] == jnp.arange(geo_count, dtype=jnp.int32)[None, None, :]).astype(
        jnp.int32
    ) * is_live[:, :, None]
    before = jnp.cumsum(onehot, axis=1) - onehot
    position = jnp.sum(before * onehot, axis=2)
    block = jnp.arange(spec_count, dtype=jnp.int32)[:, None]
    send_row = jnp.where(
        is_live == 1, block * slot_count + owners * capacity + position, spec_count * slot_count
    ).reshape(cells_dev)
    row_total = spec_count * slot_count
    source = (
        jnp.full((row_total,), cells_dev, jnp.int32)
        .at[send_row]
        .set(jnp.arange(cells_dev, dtype=jnp.int32), mode="drop")
    )
    wind_pair = jnp.stack(
        [wind_speed.reshape(cells_dev), wind_dir.reshape(cells_dev)], axis=1
    ).astype(jnp.bfloat16)
    payload = jnp.concatenate(
        [
            prop_cells,
            wind_pair,
            jnp.zeros((cells_dev, width - comp_dev - 2), jnp.bfloat16),
        ],
        axis=1,
    )
    payload = jnp.concatenate([payload, jnp.zeros((1, width), jnp.bfloat16)], axis=0)
    outgoing = jnp.take(payload, source, axis=0)
    arrived = lax.all_to_all(outgoing, BOTH, split_axis=0, concat_axis=0, tiled=True)
    arrived = arrived.reshape(spec_count, slot_count, width)
    data = arrived[:, :, :comp_dev].transpose(1, 0, 2).reshape(slot_count, spec_count * comp_dev)
    wind_rows = arrived[0, :, comp_dev]
    wind_angle = arrived[0, :, comp_dev + 1]

    coupled = lax.dot_general(
        data, pair_kernel, (((1,), (1,)), ((), ())), preferred_element_type=jnp.float32
    )
    paired = (data.astype(jnp.float32) * coupled).astype(jnp.bfloat16)
    transfer = lax.dot_general(
        paired, transfer_kernel[0], (((1,), (1,)), ((), ())), preferred_element_type=jnp.float32
    ).astype(jnp.bfloat16)
    sourced = finish(data, transfer, wind_rows, wind_angle)

    back = sourced.reshape(slot_count, spec_count, comp_dev).transpose(1, 0, 2)
    back = jnp.concatenate(
        [back, jnp.zeros((spec_count, slot_count, width - comp_dev), jnp.bfloat16)], axis=2
    ).reshape(row_total, width)
    returned = lax.all_to_all(back, BOTH, split_axis=0, concat_axis=0, tiled=True)
    gather_row = jnp.minimum(send_row, row_total - 1)
    result_cells = jnp.take(returned, gather_row, axis=0)[:, :comp_dev]
    result_cells = jnp.where(is_live.reshape(cells_dev)[:, None] == 1, result_cells, prop_cells)
    return result_cells.T.reshape(comp_dev, cells_x, cells_y)


def solution(mesh):
    placed = (
        P("spec", "geo", None),
        P("geo", None),
        P("geo", None),
        P("geo", None),
        P("geo", None),
        P("geo", None),
        P("geo", None),
        P(),
        P("geo", None, None),
    )
    return jax.shard_map(
        per_device, mesh=mesh, in_specs=placed, out_specs=P("spec", "geo", None), check_vma=False
    )
```

```python
import math

import jax
import jax.numpy as jnp
from jax import lax
from jax.sharding import PartitionSpec as P

NDIR = 36
BOTH = ("spec", "geo")


def padded_2(cells, sides, width):
    for axis, dim in sides:
        count = lax.axis_size(axis)
        ends = count - 1
        head = lax.slice_in_dim(cells, 0, width, axis=dim)
        tail = lax.slice_in_dim(cells, cells.shape[dim] - width, cells.shape[dim], axis=dim)
        cells = jnp.concatenate(
            [
                lax.ppermute(tail, axis, [(i, (i + 1) % count) for i in range(ends)]),
                cells,
                lax.ppermute(head, axis, [((i + 1) % count, i) for i in range(ends)]),
            ],
            axis=dim,
        )
    return cells


def finish(energy_bf, transfer, wind_rows, wind_angle):
    energy = energy_bf.astype(jnp.float32)
    total = jnp.mean(energy, axis=1)
    ratio = total / (1.0 + total)
    component = jnp.arange(energy_bf.shape[1], dtype=jnp.int32)
    heading = 2.0 * math.pi * ((component % NDIR).astype(jnp.float32) + 0.5) / NDIR
    angle = wind_angle.astype(jnp.float32)
    alignment = (
        jnp.cos(heading)[None, :] * jnp.cos(angle)[:, None]
        + jnp.sin(heading)[None, :] * jnp.sin(angle)[:, None]
    )
    forcing = 0.3 * wind_rows.astype(jnp.float32)[:, None] * jnp.maximum(alignment, 0.0)
    result = (
        energy * (1.0 + forcing - 0.5 * ratio[:, None])
        + 0.2 * transfer.astype(jnp.float32) / (1.0 + total)[:, None]
    )
    return result.astype(jnp.bfloat16)


def per_device(
    spectrum,
    sea_map,
    depth_factor,
    wind_speed,
    wind_dir,
    ice_mask,
    owner_map,
    pair_kernel,
    transfer_kernel,
):
    comp_dev, cells_x, cells_y = spectrum.shape
    spec_count = lax.axis_size("spec")
    geo_count = lax.axis_size("geo")
    cells_dev = cells_x * cells_y
    rows_dev = cells_dev // spec_count
    capacity = 2 * rows_dev // geo_count
    slot_count = geo_count * capacity
    width = ((comp_dev + 2 + 3) // 4) * 4

    masked = spectrum * sea_map.astype(jnp.bfloat16)[None, :, :]
    padded = padded_2(masked, (("geo", 1),), 1)
    extended = padded.astype(jnp.float32)
    component = lax.axis_index("spec") * comp_dev + jnp.arange(comp_dev, dtype=jnp.int32)
    frequency = (component // NDIR).astype(jnp.float32)
    heading = 2.0 * math.pi * ((component % NDIR).astype(jnp.float32) + 0.5) / NDIR
    cosine = jnp.cos(heading)[:, None, None]
    sine = jnp.sin(heading)[:, None, None]
    gain = (jnp.float32(1.1) ** (-0.5 * frequency))[:, None, None]
    sea_weight = sea_map.astype(jnp.float32)
    step_x = 0.7 * gain * jnp.abs(cosine) * depth_factor
    step_y = 0.7 * gain * jnp.abs(sine) * depth_factor
    centre = extended[:, 1:-1]
    west_side = extended[:, :-2]
    east_side = extended[:, 2:]
    zeros_y = jnp.zeros((comp_dev, cells_x, 1), jnp.float32)
    south_side = jnp.concatenate([zeros_y, centre[:, :, :-1]], axis=2)
    north_side = jnp.concatenate([centre[:, :, 1:], zeros_y], axis=2)
    upwind_x = jnp.where(cosine > 0, west_side, east_side)
    upwind_y = jnp.where(sine > 0, south_side, north_side)
    advected = centre - step_x * (centre - upwind_x) - step_y * (centre - upwind_y)
    propagated = (advected * sea_weight).astype(jnp.bfloat16)
    flat = propagated.reshape(comp_dev, cells_dev)

    owners = owner_map.reshape(spec_count, rows_dev)
    is_live = 1 - ice_mask.reshape(spec_count, rows_dev)
    onehot = (owners[:, :, None] == jnp.arange(geo_count, dtype=jnp.int32)[None, None, :]).astype(
        jnp.float32
    ) * is_live[:, :, None].astype(jnp.float32)
    lower = (
        jnp.arange(rows_dev, dtype=jnp.int32)[None, :] < jnp.arange(rows_dev, dtype=jnp.int32)[:, None]
    ).astype(jnp.bfloat16)
    before = jnp.einsum(
        "ij,bjo->bio", lower, onehot.astype(jnp.bfloat16), preferred_element_type=jnp.float32
    )
    position = jnp.sum(before * onehot, axis=2).astype(jnp.int32)
    slot = jnp.where(is_live == 1, owners * capacity + position, -1)
    route = (
        jnp.arange(slot_count, dtype=jnp.int32)[None, :, None] == slot[:, None, :]
    ).astype(jnp.bfloat16)
    wind_pair = jnp.stack([wind_speed.reshape(cells_dev), wind_dir.reshape(cells_dev)], axis=0)
    payload = jnp.concatenate(
        [flat, wind_pair, jnp.zeros((width - comp_dev - 2, cells_dev), jnp.bfloat16)], axis=0
    ).reshape(width, spec_count, rows_dev)
    outgoing = jnp.einsum(
        "bki,cbi->bkc", route, payload, preferred_element_type=jnp.float32
    ).astype(jnp.bfloat16)
    row_total = spec_count * slot_count
    outgoing = outgoing.reshape(row_total, width)
    arrived = lax.all_to_all(outgoing, BOTH, split_axis=0, concat_axis=0, tiled=True)
    arrived = arrived.reshape(spec_count, slot_count, width)
    data = arrived[:, :, :comp_dev].transpose(1, 0, 2).reshape(slot_count, spec_count * comp_dev)
    wind_rows = arrived[0, :, comp_dev]
    wind_angle = arrived[0, :, comp_dev + 1]

    coupled = lax.dot_general(
        data, pair_kernel, (((1,), (1,)), ((), ())), preferred_element_type=jnp.float32
    )
    paired = (data.astype(jnp.float32) * coupled).astype(jnp.bfloat16)
    transfer = lax.dot_general(
        paired, transfer_kernel[0], (((1,), (1,)), ((), ())), preferred_element_type=jnp.float32
    ).astype(jnp.bfloat16)
    sourced = finish(data, transfer, wind_rows, wind_angle)

    back = sourced.reshape(slot_count, spec_count, comp_dev).transpose(1, 0, 2)
    back = jnp.concatenate(
        [back, jnp.zeros((spec_count, slot_count, width - comp_dev), jnp.bfloat16)], axis=2
    ).reshape(row_total, width)
    returned = lax.all_to_all(back, BOTH, split_axis=0, concat_axis=0, tiled=True)
    returned = returned.reshape(spec_count, slot_count, width)[:, :, :comp_dev]
    placed_back = jnp.einsum(
        "bkc,bki->cbi", returned, route, preferred_element_type=jnp.float32
    ).astype(jnp.bfloat16).reshape(comp_dev, cells_dev)
    live_flat = is_live.reshape(cells_dev)[None, :] == 1
    result = jnp.where(live_flat, placed_back, flat)
    return result.reshape(comp_dev, cells_x, cells_y)


def solution(mesh):
    placed = (
        P("spec", "geo", None),
        P("geo", None),
        P("geo", None),
        P("geo", None),
        P("geo", None),
        P("geo", None),
        P("geo", None),
        P(),
        P("geo", None, None),
    )
    return jax.shard_map(
        per_device, mesh=mesh, in_specs=placed, out_specs=P("spec", "geo", None), check_vma=False
    )
```
